128 devices in a mesh: section: 4 (over x), expert: 32 (over z, y, core).
Axes of the slice: x: 4, y: 4, z: 4, core: 2. Of those that a mesh axis runs over, the one named last changes fastest.
Arguments:
- state: bfloat16 [2, 4, 2048, 2048], P(None, 'section', 'expert'), may hold values from -6 to 6
- norm_gain: float32 [2, 4, 2048], P(None, 'section'), may hold values from 0.1 to 1.9
- up_weight: bfloat16 [2, 4, 32, 2048, 768], P(None, 'section', 'expert'), may hold values from -0.125 to 0.125
- down_weight: bfloat16 [2, 4, 32, 768, 2048], P(None, 'section', 'expert'), may hold values from -0.21875 to 0.21875
- expert_ids: int32 [4, 2, 4, 2048, 2], P(None, None, 'section'), may hold values from 0 to 31, all different within a row; in each aligned block of 64 rows (0 to 63, 64 to 127, ..., all dimensions but the last counted through in order) at most 8 rows name the same one
- gate_values: float32 [4, 2, 4, 2048, 2], P(None, None, 'section', 'expert'), may hold values from 0.1 to 1
Outputs:
- final_state: bfloat16 [2, 4, 2048, 2048], P(None, 'section', 'expert')
- finished: bfloat16 [4, 2048, 2048], P(None, 'expert', 'section')
The draws below stay inside these ranges and needn't reach their ends.
Inputs may be any that keep to these rules, and one draw needn't show every extreme that they name: `expert_ids`: each token names two different experts. Within the 64 tokens of one index of expert (aligned blocks of 64 tokens) at one tick, slot and segment, no expert is named more than 8 times.
All inputs are finite; a program needn't handle non-finite values.
Results may differ from the reference program's by a relative error of at most 0.0095.
Values may be sent and summed in bfloat16 or wider, within the bound.
No kernel may reach another device: no remote copies, remote signals or barrier semaphores. Data moves between devices by JAX's collectives and lax.ppermute only.
A program may use at most 64 MiB of HBM per device.

```python
import math
import jax
import jax.numpy as jnp
import numpy as np
from jax import lax

D = 2048
FF = 768
TICKS = 4
TOK_DEV = 64
TOK = 2048
MOST = 8
EXPERTS = 32
N_SECTION = 4
N_EXPERT = 32


def block_levels(stream_key, dims, cuts, low, top_value):
    loudness = 1.0
    for position, blocks in cuts:
        draws = jax.random.uniform(jax.random.fold_in(jax.random.fold_in(stream_key, 6), position), (blocks,), jnp.float32, low / len(cuts), top_value / len(cuts))
        loudness = loudness * jnp.repeat(jnp.exp(draws), dims[position] // blocks).reshape((-1,) + (1,) * (len(dims) - 1 - position))
    return loudness


def routed_block(stream_key, own, number, rows, count, top, reach, lean):
    order = jax.random.permutation(stream_key, count)
    heavy_load, common = load_shares(count, rows * top, reach, lean, True), load_shares(count, rows * top, reach, lean, False)
    places = jnp.arange(count)

    def named(tallies, offset_by):
        used = int((tallies > 0).sum())
        fixed = max(1, used // 4)
        passed = fixed + (places - fixed + offset_by * (used - fixed)) % max(1, count - fixed)
        return jnp.zeros((count,), jnp.int32).at[order[jnp.where(places < fixed, places, passed)]].set(jnp.asarray(tallies, jnp.int32))

    tallies = jnp.where(number % 4 == 0, named(heavy_load, number // 4), named(common, number - number // 4 - 1))
    mixed = jax.random.permutation(jax.random.fold_in(own, 3), count)
    giver, receiver = mixed[0:count // 2 * 2:2], mixed[1:count // 2 * 2:2]
    margin = jnp.minimum(tallies[giver] - 1, reach - tallies[receiver]) // 2
    margin = jnp.where((giver == order[0]) | (receiver == order[0]) | (tallies[receiver] == 0), 0, jnp.maximum(margin, 0))
    passed = jax.random.randint(jax.random.fold_in(own, 4), (count // 2,), 0, 1 << 20) % (margin + 1)
    tallies = tallies.at[giver].add(-passed).at[receiver].add(passed)
    labels = jnp.searchsorted(jnp.cumsum(tallies), jnp.arange(rows * top), side="right").astype(jnp.int32)
    listing = labels.reshape(top, rows).T
    listing = listing[jax.random.permutation(jax.random.fold_in(own, 1), rows)]
    offset_by = jax.random.randint(jax.random.fold_in(own, 2), (rows, 1), 0, top)
    return jnp.take_along_axis(listing, (jnp.arange(top)[None, :] + offset_by) % top, axis=1)


def load_shares(amount, total, limit, skew, full):
    weights = [(1 << 20) // math.isqrt(grade ** skew) + 1 for grade in range(1, amount + 1)]
    largest = limit if full else min(limit, max(-(-total // amount), total * weights[0] // sum(weights)))
    least = 1 if total - largest >= amount - 1 else 0
    counts, surplus = [largest] + [least] * (amount - 1), total - largest - least * (amount - 1)
    while surplus > 0:
        movable = [i for i in range(1, amount) if counts[i] < largest] or [i for i in range(1, amount) if counts[i] < limit]
        whole, remaining = sum([weights[i] for i in movable]), surplus
        for i in movable:
            extra = min(limit - counts[i], max(1, remaining * weights[i] // whole), surplus)
            counts[i] = counts[i] + extra
            surplus = surplus - extra
    return np.array(counts)


def centred(rng, dims, spread, bound, split=(), kind=jnp.bfloat16):
    gain = block_levels(rng, dims, split, -0.22, 0.18) if split else 1.0
    array = jax.random.normal(rng, dims, jnp.float32) * spread * gain
    return jnp.minimum(jnp.maximum(array, -bound), bound).astype(kind)


def setup_inputs(seed: int = 0) -> dict:
    seeds = jax.random.split(jax.random.key(seed), 7)
    state = centred(seeds[0], (2, N_SECTION, TOK, D), 1.0, 6.0, ((1, 4), (2, 32)))
    norm_gain = jnp.clip(1.0 + 0.18 * jax.random.normal(seeds[1], (2, N_SECTION, D), jnp.float32), 0.1, 1.9)
    up_weight = centred(seeds[2], (2, N_SECTION, EXPERTS, D, FF), D ** -0.5, 0.125, ((1, 4), (2, 32)))
    down_weight = centred(seeds[3], (2, N_SECTION, EXPERTS, FF, D), FF ** -0.5, 0.21875, ((1, 4), (2, 32)))
    expert_ids_keys = jax.random.split(jax.random.fold_in(seeds[4], 1), TICKS * 2 * N_SECTION * TOK // TOK_DEV)
    expert_ids_turns = jax.random.permutation(jax.random.fold_in(seeds[4], 3), TICKS * 2 * N_SECTION * TOK // TOK_DEV)
    expert_ids = jax.vmap(lambda own, number: routed_block(jax.random.fold_in(seeds[4], 2), own, number, TOK_DEV, EXPERTS, 2, MOST, 2))(expert_ids_keys, expert_ids_turns).reshape((TICKS, 2, N_SECTION, TOK, 2))
    gate_values = jnp.clip(0.1 + 0.9 * jax.random.uniform(seeds[5], (TICKS, 2, N_SECTION, TOK, 2), jnp.float32) ** block_levels(seeds[5], (TICKS, 2, N_SECTION, TOK, 2), ((2, 4), (3, 32)), -0.2, 0.2), 0.1, 1.0)
    return {"state": state, "norm_gain": norm_gain, "up_weight": up_weight, "down_weight": down_weight, "expert_ids": expert_ids, "gate_values": gate_values}


def rms_norm(layer_in, norm_gain):
    widened = layer_in.astype(jnp.float32)
    scaled = lax.rsqrt(lax.optimization_barrier(jnp.mean(widened * widened, axis=-1, keepdims=True)) + 1e-06)
    return (widened * scaled * norm_gain).astype(jnp.bfloat16)

def moe_layer(layer_in, norm_gain, up_weight, down_weight, routes, gates):
    normed = rms_norm(layer_in, norm_gain)
    capacity = N_EXPERT * MOST
    all_tokens = layer_in.shape[0]

    def one_expert(accumulated, expert_index):
        matches = routes == expert_index
        token_hit = jnp.any(matches, axis=1)
        weight = lax.optimization_barrier(jnp.sum(jnp.where(matches, gates, 0.0), axis=1))
        row_index = jnp.nonzero(token_hit, size=capacity, fill_value=0)[0].astype(jnp.int32)
        live_count = jnp.sum(token_hit.astype(jnp.int32))
        is_valid = jnp.arange(capacity, dtype=jnp.int32) < live_count
        in_rows = normed[row_index]
        projected = jnp.dot(in_rows, up_weight[expert_index], preferred_element_type=jnp.float32)
        activated = jax.nn.silu(projected).astype(jnp.bfloat16)
        outputs = jnp.dot(activated, down_weight[expert_index], preferred_element_type=jnp.float32).astype(jnp.bfloat16)
        scaled = jnp.where(is_valid, weight[row_index], 0.0)[:, None] * outputs.astype(jnp.float32)
        return (accumulated.at[row_index].add(scaled), None)
    start_sum = jnp.zeros((all_tokens, layer_in.shape[1]), jnp.float32)
    expert_list = jnp.arange(up_weight.shape[0], dtype=jnp.int32)
    accumulated, _ = lax.scan(one_expert, start_sum, expert_list)
    return (layer_in.astype(jnp.float32) + accumulated).astype(jnp.bfloat16)

def apply_segment(packed):
    return moe_layer(packed[0], packed[1], packed[2], packed[3], packed[4], packed[5])

def reference(state, norm_gain, up_weight, down_weight, expert_ids, gate_values):
    current = state
    done_list = []
    for tick_index in range(TICKS):
        results = []
        for group_index in range(2):
            packed = (current[group_index], norm_gain[group_index], up_weight[group_index], down_weight[group_index], expert_ids[tick_index, group_index], gate_values[tick_index, group_index])
            results.append(lax.map(apply_segment, packed))
        first_slot, second_slot = results
        new_first = jnp.concatenate([jnp.zeros_like(first_slot[:1]), first_slot[:-1]], axis=0)
        new_second = jnp.concatenate([first_slot[-1:], second_slot[:-1]], axis=0)
        done_list.append(second_slot[-1])
        current = jnp.stack([new_first, new_second])
    return (current, jnp.stack(done_list))
```

```python
import jax
import jax.numpy as jnp
from jax import lax
from jax.experimental import pallas as pl
from jax.experimental.pallas import tpu as pltpu
from jax.sharding import PartitionSpec as P


MOST = 8
PAIRED = False
SMEM = pl.BlockSpec(memory_space=pltpu.SMEM)
VMEM = pl.BlockSpec(memory_space=pltpu.VMEM)
ANY = pl.BlockSpec(memory_space=pl.ANY)


def slot_base(ids, core):
    if not PAIRED:
        return ids * MOST
    return lax.div(ids, 2) * (2 * MOST) + lax.rem(lax.rem(ids, 2) + core, 2) * MOST


def as_square(row):
    return jnp.broadcast_to(row, (row.shape[1], row.shape[1]))


def earlier_rows(ids, axis):
    down = lax.broadcasted_iota(jnp.int32, ids.shape, 0)
    across = lax.broadcasted_iota(jnp.int32, ids.shape, 1)
    before = down < across if axis == 0 else across < down
    hits = jnp.where((ids.T == ids) & before, 1.0, 0.0)
    return jnp.sum(hits, axis=axis, keepdims=True).astype(jnp.int32)


def place(flags, sources, gain, ids, layer, slot_count):
    def body(*refs):
        flag_ref, *in_refs = refs[: 1 + len(sources)]
        gain_ref, ids_ref = refs[1 + len(sources) : 3 + len(sources)]
        outs = refs[3 + len(sources) :]
        if layer[0] == 0:
            layer_in = in_refs[0][...]
        else:
            at_start = flag_ref[0] == 1
            first = in_refs[0][...]
            if layer[1] == 0:
                layer_in = jnp.where(at_start, jnp.zeros_like(first), first)
            else:
                layer_in = jnp.where(at_start, first, in_refs[1][...])
            outs[1][...] = layer_in
        widened = layer_in.astype(jnp.float32)
        scaled = lax.rsqrt(jnp.mean(widened * widened, axis=-1, keepdims=True) + 1e-06)
        normed = (widened * scaled * gain_ref[layer[1]]).astype(jnp.bfloat16)
        row = ids_ref[layer[0], layer[1]]
        slots = slot_base(row, flag_ref[1]) + earlier_rows(as_square(row), 0)
        wanted = lax.broadcasted_iota(jnp.int32, (slot_count, slots.shape[1]), 0)
        picks = jnp.where(wanted == slots, 1.0, 0.0).astype(jnp.bfloat16)
        doubled = jnp.concatenate([normed, normed], axis=0)
        picked = jnp.dot(picks, doubled, preferred_element_type=jnp.float32)
        outs[0][...] = picked.astype(jnp.bfloat16)

    rows, width = sources[0].shape
    shapes = [jax.ShapeDtypeStruct((slot_count, width), jnp.bfloat16)]
    if layer[0] > 0:
        shapes.append(jax.ShapeDtypeStruct((rows, width), jnp.bfloat16))
    made = pl.pallas_call(
        body,
        out_shape=shapes,
        in_specs=[SMEM] + [VMEM] * (len(sources) + 2),
        out_specs=[VMEM] * len(shapes),
    )(flags, *sources, gain, ids)
    return made if layer[0] > 0 else (made[0], sources[0])


def expert_mlp(in_rows, up_weight, down_weight, group):
    rows, width = in_rows.shape
    hidden = up_weight.shape[-1]
    parts = 3
    piece = hidden // parts

    def body(in_ref, up_hbm, down_hbm, out_ref, up_ref, down_ref, sems):
        ups = [
            pltpu.make_async_copy(
                up_hbm.at[group, 0, 0, :, pl.ds(j * piece, piece)], up_ref.at[j], sems.at[j]
            )
            for j in range(parts)
        ]
        downs = [
            pltpu.make_async_copy(
                down_hbm.at[group, 0, 0, pl.ds(j * piece, piece)],
                down_ref.at[pl.ds(j * piece, piece)],
                sems.at[parts + j],
            )
            for j in range(parts)
        ]
        for copy in ups + downs:
            copy.start()
        acts = []
        for j in range(parts):
            ups[j].wait()
            value = jnp.dot(in_ref[...], up_ref[j], preferred_element_type=jnp.float32)
            acts.append((value / (1.0 + jnp.exp(-value))).astype(jnp.bfloat16))
        act = jnp.concatenate(acts, axis=1)
        for copy in downs:
            copy.wait()
        out_ref[...] = jnp.dot(
            act, down_ref[...], preferred_element_type=jnp.float32
        ).astype(jnp.bfloat16)

    return pl.pallas_call(
        body,
        out_shape=jax.ShapeDtypeStruct((rows, width), jnp.bfloat16),
        in_specs=[VMEM, ANY, ANY],
        out_specs=VMEM,
        scratch_shapes=[
            pltpu.VMEM((parts, width, piece), jnp.bfloat16),
            pltpu.VMEM((hidden, width), jnp.bfloat16),
            pltpu.SemaphoreType.DMA((2 * parts,)),
        ],
    )(in_rows, up_weight, down_weight)


def join(flags, layer_in, returned, ids, gates, layer):
    rows, width = layer_in.shape
    slot_count = returned.shape[0]

    def body(flag_ref, in_ref, back_ref, ids_ref, gate_ref, out_ref):
        square = as_square(ids_ref[layer[0], layer[1]])
        column = square.T[:, :1]
        slots = slot_base(column, flag_ref[1]) + earlier_rows(square, 1)
        wanted = lax.broadcasted_iota(jnp.int32, (slots.shape[0], slot_count), 1)
        picks = jnp.where(wanted == slots, 1.0, 0.0).astype(jnp.bfloat16)
        found = jnp.dot(picks, back_ref[...], preferred_element_type=jnp.float32)
        scaled = found * as_square(gate_ref[layer[0], layer[1]]).T[:, :1]
        total = in_ref[...].astype(jnp.float32) + (scaled[:rows] + scaled[rows:])
        out_ref[...] = total.astype(jnp.bfloat16)

    return pl.pallas_call(
        body,
        out_shape=jax.ShapeDtypeStruct((rows, width), jnp.bfloat16),
        in_specs=[SMEM] + [VMEM] * 4,
        out_specs=VMEM,
    )(flags, layer_in, returned, ids, gates)


def exchange(rows, expert_count):
    shaped = rows.reshape(expert_count, -1, rows.shape[-1])
    moved = lax.all_to_all(shaped, "expert", split_axis=0, concat_axis=0, tiled=True)
    return moved.reshape(rows.shape)


def to_next(block, sources):
    segment_count = lax.axis_size("section")
    route = [(i, (i + 1) % segment_count) for i in sources]
    return lax.ppermute(block, "section", route)


def leave(block):
    segment_count = lax.axis_size("section")
    last = segment_count - 1
    columns = block.shape[-1] // segment_count
    parts = [block[..., k * columns : (k + 1) * columns] for k in range(segment_count)]
    total = jnp.where(lax.axis_index("section") == last, parts[last], jnp.zeros_like(parts[last]))
    for k in range(last):
        total = total + lax.ppermute(parts[k], "section", [(last, k)])
    return total


def rows_of(values, owner, tok_rows):
    ticks, groups = values.shape[:2]
    if owner is not None:
        values = lax.dynamic_slice_in_dim(values, owner * tok_rows, tok_rows, 2)
    return values.transpose(0, 1, 3, 2).reshape(ticks, groups, 1, -1)


def relay(state, norm_gain, up_weight, down_weight, expert_ids, gate_values):
    expert_count = lax.axis_size("expert")
    segment_count = lax.axis_size("section")
    owner = lax.axis_index("expert")
    at_start = lax.axis_index("section") == 0
    flags = jnp.stack([at_start.astype(jnp.int32), lax.rem(owner, 2).astype(jnp.int32)])
    tok_rows = state.shape[2]
    ticks = expert_ids.shape[0]
    slot_count = expert_count * MOST
    ids = rows_of(expert_ids[:, :, 0], owner, tok_rows)
    gates = rows_of(gate_values[:, :, 0], None, tok_rows)
    everyone = range(segment_count)
    sources = [[state[0, 0]], [state[1, 0]]]
    done_list, finished = [], []
    for t in range(ticks):
        stepped = []
        for g in range(2):
            outgoing, layer_in = place(flags, sources[g], norm_gain, ids, (t, g), slot_count)
            in_rows = exchange(outgoing, expert_count)
            outputs = expert_mlp(in_rows, up_weight, down_weight, g)
            returned = exchange(outputs, expert_count)
            stepped.append(join(flags, layer_in, returned, ids, gates, (t, g)))
        first = to_next(stepped[0], everyone)
        second = to_next(stepped[1], range(segment_count - 1))
        sources = [[first], [first, second]]
        done_list.append(stepped[1])
        if t == ticks - 2:
            finished.append(leave(jnp.stack(done_list)))
            done_list = []
    finished.append(leave(jnp.stack(done_list)))
    final = jnp.stack(
        [jnp.where(at_start, jnp.zeros_like(first), first), jnp.where(at_start, first, second)]
    )
    return (final[:, None], jnp.concatenate(finished))


def solution(mesh):
    return jax.shard_map(
        relay,
        mesh=mesh,
        in_specs=(
            P(None, "section", "expert", None),
            P(None, "section", None),
            P(None, "section", "expert", None, None),
            P(None, "section", "expert", None, None),
            P(None, None, "section", None, None),
            P(None, None, "section", "expert", None),
        ),
        out_specs=(P(None, "section", "expert", None), P(None, "expert", "section")),
        check_vma=False,
    )
```
